32 devices in a mesh: row: 4 (over y, x), col: 8 (over z, core).
Axes of the slice: x: 2, y: 2, z: 4, core: 2. Of those that a mesh axis runs over, the one named last changes fastest.
Arguments:
- gradient: float32 [5120, 25600], P('row', 'col'), may hold values from -48 to 48
- previous: float32 [5120, 3840], P('row', 'col'), may hold values from -1 to 1
- root: bfloat16 [5120, 3840], P('row', 'col'), may hold values from -2.1 to 2.1
Outputs:
- statistic: float32 [5120, 3840], P('row', 'col')
- preconditioned: float32 [5120, 25600], P('row', 'col')
The draws below stay inside these ranges and needn't reach their ends.
All inputs are finite; a program needn't handle non-finite values.
Results may differ from the reference program's by a relative error of at most 0.005.
Values may be sent and summed in bfloat16 or wider, within the bound.
A program may use at most 192 MiB of HBM per device.

```python
import math
import jax
import jax.numpy as jnp
from jax import lax

WIDTH = 5120
INTER = 25600
BLOCKS = 4
HALF = 2
BLOCK_ROWS = 1280
BAND = 3840
N_COL = 8


def draw_gradient(key, part):
    subkeys = jax.random.split(jax.random.fold_in(key, 11), 3)
    row_scale = jnp.exp(jax.random.uniform(subkeys[0], (WIDTH, 1), jnp.float32, math.log(0.5), math.log(2.0)))
    col_scale = jnp.exp(jax.random.uniform(subkeys[1], (1, INTER), jnp.float32, math.log(0.5), math.log(2.0)))
    shard_place = (jnp.arange(INTER, dtype=jnp.int32)[None, :] // (INTER // N_COL)).astype(jnp.float32)
    shard_scale = jnp.exp(shard_place * (math.log(3.0) / (N_COL - 1)))
    col_scale = col_scale * shard_scale
    rough = jnp.clip(jax.random.normal(subkeys[2], (WIDTH, INTER), jnp.float32), -4.0, 4.0)
    values = rough * row_scale * col_scale
    return values.astype(jnp.float32)


def draw_root(key, part):
    subkeys = jax.random.split(jax.random.fold_in(key, 23), 2)
    spread = 0.5 / math.sqrt(WIDTH)
    noise = jnp.clip(jax.random.normal(subkeys[0], (WIDTH, BAND), jnp.float32), -4.0, 4.0) * spread
    diag_values = jnp.exp(jax.random.uniform(subkeys[1], (WIDTH, 1), jnp.float32, math.log(0.5), math.log(2.0)))
    row_place = jnp.arange(WIDTH, dtype=jnp.int32)[:, None] % BLOCK_ROWS
    col_place = jnp.arange(BAND, dtype=jnp.int32)[None, :]
    on_diagonal = (col_place == row_place).astype(jnp.float32)
    return (noise + on_diagonal * diag_values).astype(jnp.bfloat16)


def block_levels(own_key, extent, pieces, smallest, high):
    loudness = 1.0
    for dim, parts in pieces:
        steps = jax.random.uniform(jax.random.fold_in(jax.random.fold_in(own_key, 6), dim), (parts,), jnp.float32, smallest / len(pieces), high / len(pieces))
        loudness = loudness * jnp.repeat(jnp.exp(steps), extent[dim] // parts).reshape((-1,) + (1,) * (len(extent) - 1 - dim))
    return loudness


def gaussian(rng, shape, deviation, most, cuts=(), held_as=jnp.bfloat16):
    factor_of = block_levels(rng, shape, cuts, -0.22, 0.18) if cuts else 1.0
    entries = jax.random.normal(rng, shape, jnp.float32) * deviation * factor_of
    return jnp.minimum(jnp.maximum(entries, -most), most).astype(held_as)


def setup_inputs(seed: int = 0) -> dict:
    key_of = jax.random.split(jax.random.key(seed), 4)
    return {
        "gradient": draw_gradient(jax.random.fold_in(key_of[3], 71), 0),
        "previous": gaussian(key_of[1], (WIDTH, BAND), 0.2, 1.0, ((0, 4), (1, 8)), jnp.float32),
        "root": draw_root(jax.random.fold_in(key_of[3], 71), 0),
    }


def reference(gradient, previous, root):
    rounded = gradient.astype(jnp.bfloat16).astype(jnp.float32)
    blocks = rounded.reshape(BLOCKS, BLOCK_ROWS, INTER)
    gram_tiles = []
    for offset in range(HALF + 1):
        shifted = jnp.roll(blocks, offset, axis=0)
        gram_tiles.append(jnp.einsum("irn,isn->irs", blocks, shifted, precision=lax.Precision.HIGHEST))
    gram_band = jnp.stack(gram_tiles, axis=2).reshape(WIDTH, BAND)
    statistic = 0.9 * previous + (0.1 / INTER) * gram_band
    root_tiles = root.astype(jnp.float32).reshape(BLOCKS, BLOCK_ROWS, HALF + 1, BLOCK_ROWS)
    applied = jnp.zeros((BLOCKS, BLOCK_ROWS, INTER), jnp.float32)
    for offset in range(HALF + 1):
        shifted = jnp.roll(blocks, offset, axis=0)
        applied = applied + jnp.einsum("irs,isn->irn", root_tiles[:, :, offset, :], shifted, precision=lax.Precision.HIGHEST)
    for offset in range(1, HALF):
        shifted = jnp.roll(blocks, -offset, axis=0)
        mirrored = jnp.roll(root_tiles[:, :, offset, :], -offset, axis=0)
        applied = applied + jnp.einsum("isr,isn->irn", mirrored, shifted, precision=lax.Precision.HIGHEST)
    return statistic, applied.reshape(WIDTH, INTER)
```

```python
import jax
import jax.numpy as jnp
from jax import lax
from jax.sharding import PartitionSpec as P

LANES = 128


def passed_along(x, axis, by):
    count = lax.axis_size(axis)
    return lax.ppermute(x, axis, [(i, (i + by) % count) for i in range(count)])


def swapped(x, axis, bit):
    return lax.ppermute(x, axis, [(i, i ^ bit) for i in range(lax.axis_size(axis))])


def contract_rows(left, right):
    return lax.dot_general(
        left, right, (((0,), (0,)), ((), ())), preferred_element_type=jnp.float32
    )


def contract_cols(left, right):
    return lax.dot_general(
        left, right, (((1,), (1,)), ((), ())), preferred_element_type=jnp.float32
    )


def finished(previous, gram_tiles, columns):
    gram_band = jnp.concatenate([tile.astype(jnp.bfloat16) for tile in gram_tiles], axis=1)
    own_share = lax.psum_scatter(gram_band, "col", scatter_dimension=1, tiled=True)
    return 0.9 * previous + 0.1 / columns * own_share.astype(jnp.float32)


def ring(gradient, previous, root):
    block_rows = gradient.shape[0]
    half_cycle = lax.axis_size("row") // 2
    own_rows = gradient.astype(jnp.bfloat16)
    full_band = lax.all_gather(root, "col", axis=1, tiled=True)

    def own_tile(offset):
        return full_band[:, offset * block_rows : (offset + 1) * block_rows]

    gram_tiles = []
    moving = own_rows
    applied = jnp.zeros(own_rows.shape, jnp.float32)
    for offset in range(half_cycle + 1):
        if offset > 0:
            moving = passed_along(moving, "row", 1)
        gram_tiles.append(contract_cols(own_rows, moving))
        applied = applied + jnp.dot(own_tile(offset), moving, preferred_element_type=jnp.float32)
    for offset in range(1, half_cycle):
        partial_term = contract_rows(own_tile(offset), own_rows)
        applied = applied + passed_along(partial_term.astype(jnp.bfloat16), "row", -offset).astype(
            partial_term.dtype
        )
    columns = gradient.shape[1] * lax.axis_size("col")
    return finished(previous, gram_tiles, columns), applied


def square(gradient, previous, root, pieces):
    rows, width = gradient.shape
    piece = width // pieces
    odd = lax.axis_index("row") % 2 == 1
    own = [gradient[:, c * piece : (c + 1) * piece].astype(jnp.bfloat16) for c in range(pieces)]
    full_band = lax.all_gather(root, "col", axis=1, tiled=True)
    tiles = [full_band[:, k * rows : (k + 1) * rows] for k in range(3)]

    by_two = [swapped(own[c], "row", 2) for c in range(pieces)]
    across = pieces // 2
    late = list(range(pieces - across, pieces))
    even_order = own + [by_two[c] for c in late]
    odd_order = [own[late[0]]] + by_two + [own[c] for c in late[1:]]
    landed = [
        swapped(jnp.where(odd, odd_order[k], even_order[k]), "row", 1)
        for k in range(pieces + across)
    ]
    by_one = [jnp.where(odd, landed[c], landed[c + 1]) for c in range(pieces)]
    ahead = [swapped(by_one[c], "row", 2) for c in range(pieces - across)]
    ahead.append(jnp.where(odd, landed[pieces], landed[0]))
    ahead += landed[pieces + 1 :]

    half = rows // 2
    side = lax.axis_index("col") % 2
    mine = lax.dynamic_slice_in_dim(tiles[1], side * half, half, 0)
    mine = passed_along(mine, "row", -1)
    other = swapped(mine, "col", 1)
    mirrored = jnp.where(
        side == 0,
        jnp.concatenate([mine, other], axis=0),
        jnp.concatenate([other, mine], axis=0),
    )

    whole = [jnp.concatenate(parts, axis=1) for parts in (own, by_one, by_two, ahead)]
    gram_tiles = [contract_cols(whole[0], whole[k]) for k in range(3)]
    applied = jnp.dot(tiles[0], whole[0], preferred_element_type=jnp.float32)
    applied = applied + jnp.dot(tiles[2], whole[2], preferred_element_type=jnp.float32)
    applied = applied + jnp.dot(tiles[1], whole[1], preferred_element_type=jnp.float32)
    applied = applied + contract_rows(mirrored, whole[3])
    columns = width * lax.axis_size("col")
    return finished(previous, gram_tiles, columns), applied


def local(gradient, previous, root):
    width = gradient.shape[1]
    fitting = [n for n in (5, 4, 3, 2) if width % (n * LANES) == 0]
    if lax.axis_size("row") == 4 and lax.axis_size("col") % 2 == 0 and fitting:
        return square(gradient, previous, root, fitting[0])
    return ring(gradient, previous, root)


def solution(mesh):
    in_specs = (P("row", "col"), P("row", "col"), P("row", "col"))
    out_specs = (P("row", "col"), P("row", "col"))
    return jax.shard_map(local, mesh=mesh, in_specs=in_specs, out_specs=out_specs, check_vma=False)
```
